32 devices in a mesh: dp: 8 (over z, core), space: 4 (over y, x).
Axes of the slice: x: 2, y: 2, z: 4, core: 2. Of those that a mesh axis runs over, the one named last changes fastest.
Arguments:
- volume: bfloat16 [8, 8, 32, 32, 128], P('dp', 'space'), may hold values from -6 to 6
- filter_one: bfloat16 [3, 3, 3, 128, 128], replicated, may hold values from -0.109375 to 0.109375
- filter_two: bfloat16 [3, 3, 3, 128, 128], replicated, may hold values from -0.109375 to 0.109375
- cotangent: bfloat16 [8, 8, 32, 32, 128], P('dp', 'space'), may hold values from -6 to 6
Outputs:
- block_out: bfloat16 [8, 8, 32, 32, 128], P('dp', 'space')
- input_grad: bfloat16 [8, 8, 32, 32, 128], P('dp', 'space')
- grad_one: float32 [3, 3, 3, 128, 128], replicated
- grad_two: float32 [3, 3, 3, 128, 128], replicated
The draws below stay inside these ranges and needn't reach their ends.
All inputs are finite; a program needn't handle non-finite values.
Results may differ from the reference program's by a relative error of at most 0.0031.
Values may be sent and summed in bfloat16 or wider, within the bound.
No kernel may reach another device: no remote copies, remote signals or barrier semaphores. Data moves between devices by JAX's collectives and lax.ppermute only.
A program may use at most 128 MiB of HBM per device.

```python
import math
import jax
import jax.numpy as jnp
from jax import lax

CHANS = 128
SIDE = 32
DEPTH = 8
SAMPLES = 8


def shard_levels(own_key, extent, pieces, low, top_value):
    loudness = 1.0
    for dim, blocks in pieces:
        heights = jax.random.uniform(jax.random.fold_in(jax.random.fold_in(own_key, 6), dim), (blocks,), jnp.float32, low / len(pieces), top_value / len(pieces))
        loudness = loudness * jnp.repeat(jnp.exp(heights), extent[dim] // blocks).reshape((-1,) + (1,) * (len(extent) - 1 - dim))
    return loudness


def scatter_about(stream_key, shape, scale, reach, pieces=(), dtype=jnp.bfloat16):
    factor_of = shard_levels(stream_key, shape, pieces, -0.22, 0.18) if pieces else 1.0
    values = jax.random.normal(stream_key, shape, jnp.float32) * scale * factor_of
    return jnp.minimum(jnp.maximum(values, -reach), reach).astype(dtype)


def setup_inputs(seed: int = 0) -> dict:
    seeds = jax.random.split(jax.random.key(seed), 5)
    volume = scatter_about(seeds[0], (SAMPLES, DEPTH, SIDE, SIDE, CHANS), 1.0, 6.0, ((0, 8), (1, 4)))
    filter_one = scatter_about(seeds[1], (3, 3, 3, CHANS, CHANS), (27 * CHANS) ** -0.5, 0.109375)
    filter_two = scatter_about(seeds[2], (3, 3, 3, CHANS, CHANS), (27 * CHANS) ** -0.5, 0.109375)
    cotangent = scatter_about(seeds[3], (SAMPLES, DEPTH, SIDE, SIDE, CHANS), 1.0, 6.0, ((0, 8), (1, 4)))
    return {"volume": volume, "filter_one": filter_one, "filter_two": filter_two, "cotangent": cotangent}


def convolve(field, filters):
    return lax.conv_general_dilated(field, filters, (1, 1, 1), 'SAME', dimension_numbers=('NDHWC', 'DHWIO', 'NDHWC'), precision=lax.Precision.HIGHEST)

def flipped(filters):
    return jnp.transpose(filters[::-1, ::-1, ::-1], (0, 1, 2, 4, 3))

def filter_grad(field, grad, filters):
    _, pull = jax.vjp(lambda w: convolve(field, w), filters)
    return pull(grad)[0]

def reference(volume, filter_one, filter_two, cotangent):
    x_full = volume.astype(jnp.float32)
    w_one = filter_one.astype(jnp.float32)
    w_two = filter_two.astype(jnp.float32)
    g_full = cotangent.astype(jnp.float32)
    pre = convolve(x_full, w_one)
    act = jax.nn.silu(pre).astype(jnp.bfloat16).astype(jnp.float32)
    block_out = (x_full + convolve(act, w_two)).astype(jnp.bfloat16)
    act_grad = convolve(g_full, flipped(w_two))
    sigma = jax.nn.sigmoid(pre)
    pre_grad = (act_grad * sigma * (1.0 + pre * (1.0 - sigma))).astype(jnp.bfloat16).astype(jnp.float32)
    input_grad = (g_full + convolve(pre_grad, flipped(w_one))).astype(jnp.bfloat16)
    factor = 1.0 / math.sqrt(SAMPLES * DEPTH * SIDE * SIDE)
    grad_two = filter_grad(act, g_full, w_two) * factor
    grad_one = filter_grad(x_full, pre_grad, w_one) * factor
    return (block_out, input_grad, grad_one, grad_two)
```

```python
import functools
import math
import jax
import jax.numpy as jnp
from jax import lax
from jax.experimental import pallas as pl
from jax.experimental.pallas import tpu as pltpu
from jax.sharding import PartitionSpec as P

AXES = ("dp", "space")
VMEM = pl.BlockSpec(memory_space=pltpu.VMEM)
SMEM = pl.BlockSpec(memory_space=pltpu.SMEM)


def divisor(n, most):
    return max(d for d in range(1, most + 1) if n % d == 0)


def factors(n):
    out = []
    while n > 1:
        f = 4 if n % 4 == 0 else 2
        out.append(f)
        n //= f
    return out


def stages_of(dp, space):
    stages = [(space, 2)]
    stride = 1
    for f in factors(space):
        stages.append((stride, f))
        stride *= f
    stride = 2 * space
    for f in factors(dp // 2):
        stages.append((stride, f))
        stride *= f
    return stages


def swap_to(value, stride, size, offset, devices):
    def partner(rank):
        digit = (rank // stride) % size
        return rank + ((digit ^ offset) - digit) * stride

    return lax.ppermute(value, AXES, [(rank, partner(rank)) for rank in range(devices)])


def blocks(count, most, body):
    step = divisor(count, most)

    def one(i, carry):
        body(pl.multiple_of(i * step, step), step)
        return carry

    lax.fori_loop(0, count // step, one, 0)


def scatter_kernel(size, arrived, piece, digit_ref, *refs):
    kept, got = refs[0], refs[1 : 1 + arrived]
    keep, sends = refs[1 + arrived], refs[2 + arrived :]
    digit = digit_ref[0]
    for offset in range(size):
        base = (digit ^ offset) * piece if size > 1 else 0
        target = keep if offset == 0 else sends[offset - 1]

        def move(at, step, base=base, target=target):
            value = kept[pl.ds(base + at, step)]
            for other in got:
                value = value + other[pl.ds(base + at, step)].astype(jnp.float32)
            target[pl.ds(at, step)] = value.astype(target.dtype)

        blocks(piece, 32, move)


def scatter_step(kept, got, digit, size, wire=jnp.bfloat16):
    piece = kept.shape[0] // size
    shape = (piece,) + kept.shape[1:]
    last = jnp.bfloat16 if size == 1 else jnp.float32
    return pl.pallas_call(
        functools.partial(scatter_kernel, size, len(got), piece),
        out_shape=[jax.ShapeDtypeStruct(shape, last)]
        + [jax.ShapeDtypeStruct(shape, wire)] * (size - 1),
        in_specs=[SMEM] + [VMEM] * (1 + len(got)),
        out_specs=[VMEM] * size,
        name="scatter_step",
    )(digit.reshape(1), kept, *got)


def gather_kernel(size, piece, factor, digit_ref, *refs):
    out = refs[size]
    digit = digit_ref[0]
    for offset in range(size):
        base = (digit ^ offset) * piece if size > 1 else 0

        def move(at, step, base=base, source=refs[offset]):
            value = source[pl.ds(at, step)]
            if factor is not None:
                value = value.astype(jnp.float32) * factor
            out[pl.ds(base + at, step)] = value

        blocks(piece, 32, move)


def gather_step(pieces, digit, factor=None):
    size, piece = len(pieces), pieces[0].shape[0]
    dtype = jnp.bfloat16 if factor is None else jnp.float32
    return pl.pallas_call(
        functools.partial(gather_kernel, size, piece, factor),
        out_shape=jax.ShapeDtypeStruct((size * piece,) + pieces[0].shape[1:], dtype),
        in_specs=[SMEM] + [VMEM] * size,
        out_specs=VMEM,
        name="gather_step",
    )(digit.reshape(1), *pieces)


def total(terms, factor):
    dp, space = lax.axis_size("dp"), lax.axis_size("space")
    devices = dp * space
    rank = lax.axis_index("dp") * space + lax.axis_index("space")
    stages = stages_of(dp, space)
    digits = [(rank // stride) % size for stride, size in stages]
    count = terms.shape[0]
    kept, got = jnp.pad(terms, ((0, -count % devices), (0, 0), (0, 0))), []
    for (stride, size), digit in zip(stages, digits):
        wire = jnp.float32 if stride == space else jnp.bfloat16
        kept, *sends = scatter_step(kept, got, digit, size, wire)
        got = [swap_to(s, stride, size, i + 1, devices) for i, s in enumerate(sends)]
    (mine,) = scatter_step(kept, got, digits[0], 1)
    for i in reversed(range(len(stages))):
        stride, size = stages[i]
        pieces = [mine] + [swap_to(mine, stride, size, o, devices) for o in range(1, size)]
        mine = gather_step(pieces, digits[i], factor if i == 0 else None)
    return mine[:count]


def with_halo(cells, sides, width):
    for axis, dim in sides:
        count = lax.axis_size(axis)
        ends = count - 1
        head = lax.slice_in_dim(cells, 0, width, axis=dim)
        tail = lax.slice_in_dim(cells, cells.shape[dim] - width, cells.shape[dim], axis=dim)
        cells = jnp.concatenate(
            [
                lax.ppermute(tail, axis, [(i, (i + 1) % count) for i in range(ends)]),
                cells,
                lax.ppermute(head, axis, [((i + 1) % count, i) for i in range(ends)]),
            ],
            axis=dim,
        )
    return cells


def columns(padded, planes):
    side = padded.shape[1]
    wide = jnp.pad(padded, ((0, 0), (1, 1), (1, 1), (0, 0)))
    pieces = []
    for kz in range(3):
        for ky in range(3):
            for kx in range(3):
                pieces.append(wide[kz : kz + planes, ky : ky + side, kx : kx + side, :])
    joined = jnp.concatenate(pieces, axis=-1)
    return joined.reshape(planes * side * side, joined.shape[-1])


def matmul(left, right):
    return jnp.dot(left, right, preferred_element_type=jnp.float32)


def outer_sum(cols, grad):
    return lax.dot_general(cols, grad, (((0,), (0,)), ((), ())), preferred_element_type=jnp.float32)


def local(volume, filter_one, filter_two, cotangent):
    field = volume[0]
    grad_out = cotangent[0]
    planes, side, chans = (field.shape[0], field.shape[1], field.shape[3])
    cells = planes * side * side
    w_one = filter_one.reshape(27 * chans, chans)
    w_two = filter_two.reshape(27 * chans, chans)
    back_one = jnp.transpose(filter_one[::-1, ::-1, ::-1], (0, 1, 2, 4, 3)).reshape(
        27 * chans, chans
    )
    back_two = jnp.transpose(filter_two[::-1, ::-1, ::-1], (0, 1, 2, 4, 3)).reshape(
        27 * chans, chans
    )
    padded_x = with_halo(field, (("space", 0),), 1)
    cols_x = columns(padded_x, planes)
    pre = matmul(cols_x, w_one).reshape(planes, side, side, chans)
    act = jax.nn.silu(pre).astype(jnp.bfloat16)
    padded_a = with_halo(act, (("space", 0),), 1)
    cols_a = columns(padded_a, planes)
    second = matmul(cols_a, w_two)
    block_out = (field.reshape(cells, chans).astype(jnp.float32) + second).astype(jnp.bfloat16)
    padded_g = with_halo(grad_out, (("space", 0),), 1)
    cols_g = columns(padded_g, planes)
    act_grad = matmul(cols_g, back_two).reshape(planes, side, side, chans)
    sigma = jax.nn.sigmoid(pre)
    pre_grad = (act_grad * sigma * (1.0 + pre * (1.0 - sigma))).astype(jnp.bfloat16)
    padded_d = with_halo(pre_grad, (("space", 0),), 1)
    flat_g = grad_out.reshape(cells, chans)
    input_grad = (flat_g.astype(jnp.float32) + matmul(columns(padded_d, planes), back_one)).astype(
        jnp.bfloat16
    )
    factor = 1.0 / math.sqrt(lax.axis_size("dp") * lax.axis_size("space") * cells)
    term_two = outer_sum(act.reshape(cells, chans), cols_g).reshape(chans, 3, 3, 3, chans)
    term_two = jnp.transpose(term_two[:, ::-1, ::-1, ::-1], (1, 2, 3, 0, 4)).reshape(27 * chans, chans)
    term_one = outer_sum(cols_x, pre_grad.reshape(cells, chans))
    grads = total(jnp.concatenate([term_one, term_two], 0).reshape(-1, 8, chans), factor)
    grad_one, grad_two = grads.reshape(2, 3, 3, 3, chans, chans)
    return (
        block_out.reshape(1, planes, side, side, chans),
        input_grad.reshape(1, planes, side, side, chans),
        grad_one,
        grad_two,
    )


def solution(mesh):
    placed = (P("dp", "space", None, None, None), P(), P(), P("dp", "space", None, None, None))
    return jax.shard_map(
        local,
        mesh=mesh,
        in_specs=placed,
        out_specs=(
            P("dp", "space", None, None, None),
            P("dp", "space", None, None, None),
            P(),
            P(),
        ),
        check_vma=False,
    )
```

```python
import functools
import math

import jax
import jax.numpy as jnp
from jax import lax
from jax.experimental import pallas as pl
from jax.experimental.pallas import tpu as pltpu
from jax.sharding import PartitionSpec as P

AXES = ("dp", "space")
LIMIT = 20 * 2**20
VMEM = pl.BlockSpec(memory_space=pltpu.VMEM)
SMEM = pl.BlockSpec(memory_space=pltpu.SMEM)
ANY = pl.BlockSpec(memory_space=pl.ANY)
BF16, F32 = jnp.bfloat16, jnp.float32


def divisor(n, most):
    return max(d for d in range(1, most + 1) if n % d == 0)


def factors(n):
    out = []
    while n > 1:
        f = 4 if n % 4 == 0 else 2
        out.append(f)
        n //= f
    return out


def swap_to(value, stride, size, offset, devices):
    def partner(rank):
        digit = (rank // stride) % size
        return rank + ((digit ^ offset) - digit) * stride

    return lax.ppermute(value, AXES, [(rank, partner(rank)) for rank in range(devices)])


def call(kernel, outs, args, scalars=(), order=(), scratch=(), flops=0, name=None):
    size = sum(a.size * a.dtype.itemsize for a in args) + sum(o.size * o.dtype.itemsize for o in outs)
    used = len(scalars) + len(args)

    def body(*refs):
        kernel(*refs[:used], *refs[used + len(order) :])

    return pl.pallas_call(
        body,
        out_shape=list(outs),
        in_specs=[SMEM] * len(scalars) + [VMEM] * len(args) + [ANY] * len(order),
        out_specs=[VMEM] * len(outs),
        scratch_shapes=list(scratch),
        cost_estimate=pl.CostEstimate(flops=flops, bytes_accessed=size, transcendentals=0),
        compiler_params=pltpu.CompilerParams(vmem_limit_bytes=LIMIT),
        name=name,
    )(*[s.reshape(1) for s in scalars], *args, *order)


def blocks(count, most, body):
    step = divisor(count, most)

    def one(i, carry):
        body(pl.multiple_of(i * step, step), step)
        return carry

    lax.fori_loop(0, count // step, one, 0)


def copy(source, target):
    target[...] = source[...]


def tiles(count, chans, dtype):
    return jax.ShapeDtypeStruct((count, 8, chans), dtype)


def join_kernel(size, pairs, digit_ref, *refs):
    given, rest = refs[: 2 * pairs], refs[2 * pairs :]
    part = given[0].shape[0] // size
    digit = digit_ref[0]
    for offset in range(size):
        target = rest[offset]
        for pair in range(pairs):
            kept, got = given[2 * pair], given[2 * pair + 1]

            def move(at, step, kept=kept, got=got, target=target, pair=pair, offset=offset):
                here = pl.ds((digit ^ offset) * part + at, step)
                value = kept[here] + got[here].astype(F32)
                target[pl.ds(pair * part + at, step)] = value.astype(target.dtype)

            blocks(part, 32, move)
        spare = target.shape[0] - pairs * part
        if spare:
            target[pl.ds(pairs * part, spare)] = jnp.zeros((spare,) + target.shape[1:], target.dtype)


def scatter_kernel(size, arrived, carried, digit_ref, *refs):
    kept, got = refs[0], refs[1 : 1 + arrived]
    moved = refs[1 + arrived : 1 + arrived + carried]
    outs = refs[1 + arrived + carried :]
    for source, target in zip(moved, outs[size:]):
        copy(source, target)
    digit = digit_ref[0]
    piece = outs[0].shape[0]
    for offset in range(size):
        base = (digit ^ offset) * piece if size > 1 else 0

        def move(at, step, base=base, target=outs[offset]):
            value = kept[pl.ds(base + at, step)]
            for other in got:
                value = value + other[pl.ds(base + at, step)].astype(F32)
            target[pl.ds(at, step)] = value.astype(target.dtype)

        blocks(piece, 32, move)


def gather_kernel(size, digit_ref, *refs):
    out = refs[size]
    digit = digit_ref[0]
    piece = refs[0].shape[0]
    for offset in range(size):
        base = (digit ^ offset) * piece

        def move(at, step, base=base, source=refs[offset]):
            out[pl.ds(base + at, step)] = source[pl.ds(at, step)]

        blocks(piece, 32, move)


def finish_kernel(size, part, factor, core_ref, digit_ref, *refs):
    outs = refs[2 * size :]
    half = size * part
    for side in range(2):
        core = core_ref[0] ^ side
        for offset in range(size):
            source = refs[side * size + offset]
            for i, out in enumerate(outs):

                def move(at, step, source=source, out=out, core=core, offset=offset, i=i):
                    to = core * half + (digit_ref[0] ^ offset) * part + at
                    out[pl.ds(to, step)] = source[pl.ds(i * part + at, step)].astype(F32) * factor

                blocks(part, 32, move)


def turn_kernel(one_ref, two_ref, one_out, two_out):
    for source, target in ((one_ref, one_out), (two_ref, two_out)):
        chans = source.shape[1]
        taps = source.shape[0] // chans

        def turn(tap, carry, source=source, target=target, taps=taps, chans=chans):
            block = source[pl.ds(pl.multiple_of((taps - 1 - tap) * chans, chans), chans), :]
            to = pl.ds(pl.multiple_of(tap * chans, chans), chans)
            target[to, :] = jnp.transpose(block.astype(F32)).astype(BF16)
            return carry

        lax.fori_loop(0, taps, turn, 0, unroll=3)


def spread(source, plane, wide, slot, side):
    chans = source.shape[-1]
    step = 8 * side
    edge = jnp.zeros((side, 3 * chans), BF16)
    wide[slot, pl.ds(0, side), :] = edge
    wide[slot, pl.ds(side + source.shape[1], side), :] = edge
    column = lax.broadcasted_iota(jnp.int32, (step, chans), 0) % side

    def some(i, carry):
        at = pl.multiple_of(i * step, step)
        value = source[plane, pl.ds(at, step), :]
        full = value.astype(F32)
        left = jnp.where(column == 0, 0.0, pltpu.roll(full, 1, 0))
        right = jnp.where(column == side - 1, 0.0, pltpu.roll(full, step - 1, 0))
        to = pl.ds(pl.multiple_of(at + side, side), step)
        wide[slot, to, pl.ds(0, chans)] = left.astype(BF16)
        wide[slot, to, pl.ds(chans, chans)] = value
        wide[slot, to, pl.ds(2 * chans, chans)] = right.astype(BF16)
        return carry

    lax.fori_loop(0, source.shape[1] // step, some, 0)


def spread_all(own, low, high, wide, side):
    planes = own.shape[0]
    spread(low, 0, wide, 0, side)
    for plane in range(planes):
        spread(own, plane, wide, plane + 1, side)
    spread(high, 0, wide, planes + 1, side)


def conv(wide, weights, side, finish):
    slots, rows = wide.shape[0], wide.shape[1] - 2 * side
    planes, chans = slots - 2, weights.shape[1]
    depth = 9 * chans
    step = STEP * side
    empty = jnp.zeros((depth, chans), BF16)

    def some(i, carry):
        at = pl.multiple_of(i * step, step)
        left = jnp.concatenate(
            [
                wide[slot, pl.ds(pl.multiple_of(at + dy * side, side), step), :]
                for slot in range(slots)
                for dy in range(3)
            ],
            axis=-1,
        )
        right = jnp.concatenate(
            [
                jnp.concatenate(
                    [
                        weights[pl.ds((slot - out) * depth, depth), :] if 0 <= slot - out <= 2 else empty
                        for out in range(planes)
                    ],
                    axis=-1,
                )
                for slot in range(slots)
            ],
            axis=0,
        )
        sums = jnp.dot(left, right, preferred_element_type=F32)
        for plane in range(planes):
            finish(plane, pl.ds(at, step), sums[:, plane * chans : (plane + 1) * chans])
        return carry

    lax.fori_loop(0, rows // step, some, 0)


def silu_kernel(side, own, low, high, weights, wide, act, first, last, slope):
    spread_all(own, low, high, wide, side)

    def finish(plane, at, pre):
        sigma = 1.0 / (1.0 + jnp.exp(-pre))
        value = (pre * sigma).astype(BF16)
        act[plane, at, :] = value
        if plane == 0:
            first[0, at, :] = value
        if plane == own.shape[0] - 1:
            last[0, at, :] = value
        slope[plane, at, :] = sigma * (1.0 + pre * (1.0 - sigma))

    conv(wide, weights, side, finish)


def slope_kernel(side, own, low, high, weights, slope, wide, grad):
    spread_all(own, low, high, wide, side)

    def finish(plane, at, part):
        grad[plane, at, :] = (part * slope[plane, at, :]).astype(BF16)

    conv(wide, weights, side, finish)


def add_kernel(side, own, low, high, weights, base, out, wide):
    spread_all(own, low, high, wide, side)

    def finish(plane, at, part):
        out[plane, at, :] = (base[plane, at, :].astype(F32) + part).astype(BF16)

    conv(wide, weights, side, finish)


def outer_kernel(turned, core_ref, own, wide, keep, send, flat, sums, full):
    planes, rows, chans = own.shape
    side = (wide.shape[1] - rows) // 2
    for plane in range(planes):
        for i in range(rows // 256):
            value = own[plane, pl.ds(i * 256, 256), :].astype(F32)
            flat[pl.ds(plane * chans, chans), pl.ds(i * 256, 256)] = jnp.transpose(value).astype(BF16)
    for slot in range(planes + 2):
        begin, end = max(0, slot - 2), min(planes, slot + 1)
        right = jnp.concatenate([wide[slot, pl.ds(dy * side, rows), :] for dy in range(3)], axis=-1)
        left = flat[pl.ds(begin * chans, (end - begin) * chans), :]
        product = jnp.dot(left, right, preferred_element_type=F32)
        for plane in range(begin, end):
            part = product[(plane - begin) * chans : (plane - begin + 1) * chans]
            sums[slot - plane] = part if plane == 0 else sums[slot - plane] + part
    deep = chans // 8
    for kz in range(3):
        for tap in range(9):
            part = sums[kz, :, pl.ds(tap * chans, chans)]
            index = kz * 9 + tap if turned else 26 - kz * 9 - tap
            part = jnp.transpose(part) if turned else part
            full[pl.ds(index * deep, deep)] = part.reshape(deep, 8, chans)
    half = keep.shape[0]
    for target, core in ((keep, core_ref[0]), (send, 1 - core_ref[0])):

        def move(at, step, target=target, core=core):
            target[pl.ds(at, step)] = full[pl.ds(core * half + at, step)].astype(target.dtype)

        blocks(half, 32, move)


def edge_kernel(cells, first, last):
    first[0] = cells[0]
    last[0] = cells[cells.shape[0] - 1]


def from_sides(first, last):
    count = lax.axis_size("space")
    low = lax.ppermute(last, "space", [(i, i + 1) for i in range(count - 1)])
    high = lax.ppermute(first, "space", [(i + 1, i) for i in range(count - 1)])
    return low, high


STEP = 32


def local(volume, filter_one, filter_two, cotangent):
    _, planes, side, _, chans = volume.shape
    rows = side * side
    dp, space = lax.axis_size("dp"), lax.axis_size("space")
    devices = dp * space
    rank = lax.axis_index("dp") * space + lax.axis_index("space")
    core = (rank // space) % 2
    field = volume.reshape(planes, rows, chans)
    grad_out = cotangent.reshape(planes, rows, chans)
    w_one = filter_one.reshape(-1, chans)
    w_two = filter_two.reshape(-1, chans)
    slab = jax.ShapeDtypeStruct((planes, rows, chans), BF16)
    plane = jax.ShapeDtypeStruct((1, rows, chans), BF16)
    wide = jax.ShapeDtypeStruct((planes + 2, rows + 2 * side, 3 * chans), BF16)
    flops = 2 * planes * rows * 27 * chans * chans
    half = 27 * chans // 16

    stages, stride = [], 1
    for size in factors(space):
        stages.append((stride, size))
        stride *= size
    stride = 2 * space
    for size in factors(dp // 2):
        stages.append((stride, size))
        stride *= size
    digits = [(rank // stride) % size for stride, size in stages]

    x_edges = call(edge_kernel, [plane] * 2, [field], name="edges_x")
    low_x, high_x = from_sides(*x_edges)
    back_one, back_two = call(
        turn_kernel,
        [jax.ShapeDtypeStruct(w_one.shape, BF16)] * 2,
        [w_one, w_two],
        order=x_edges,
        name="turn",
    )
    g_edges = call(edge_kernel, [plane] * 2, [grad_out], order=[back_two], name="edges_g")
    low_g, high_g = from_sides(*g_edges)
    wide_x, act, act_first, act_last, slope = call(
        functools.partial(silu_kernel, side),
        [wide, slab, plane, plane, jax.ShapeDtypeStruct(slab.shape, F32)],
        [field, low_x, high_x, w_one],
        flops=flops,
        name="conv_pre",
    )
    low_a, high_a = from_sides(act_first, act_last)
    wide_g, grad_pre = call(
        functools.partial(slope_kernel, side),
        [wide, slab],
        [grad_out, low_g, high_g, back_two, slope],
        flops=flops,
        name="conv_act_grad",
    )

    def outer(turned, own, spread_out, order, name):
        return call(
            functools.partial(outer_kernel, turned),
            [tiles(half, chans, F32)] * 2,
            [own, spread_out],
            scalars=[core],
            order=order,
            scratch=[
                pltpu.VMEM((planes * chans, rows), BF16),
                pltpu.VMEM((3, chans, 9 * chans), F32),
                pltpu.VMEM((2 * half, 8, chans), F32),
            ],
            flops=flops,
            name=name,
        )

    keep_two, send_two = outer(False, act, wide_g, [], "outer_two")
    got_two = swap_to(send_two, space, 2, 1, devices)
    keep_one, send_one = outer(True, grad_pre, wide_x, [send_two], "outer_one")
    got_one = swap_to(send_one, space, 2, 1, devices)

    def conv_out(order):
        return call(
            functools.partial(add_kernel, side),
            [slab],
            [act, low_a, high_a, w_two, field],
            order=order,
            scratch=[pltpu.VMEM(wide.shape, BF16)],
            flops=flops,
            name="conv_out",
        )[0]

    def conv_in(order, low_d, high_d):
        return call(
            functools.partial(add_kernel, side),
            [slab],
            [grad_pre, low_d, high_d, back_one, grad_out],
            order=order,
            scratch=[pltpu.VMEM(wide.shape, BF16)],
            flops=flops,
            name="conv_in",
        )[0]

    (stride, size), digit = stages[0], digits[0]
    rest = devices // 2 // size
    piece = -(-2 * half // size // rest) * rest
    kept, *sends = call(
        functools.partial(join_kernel, size, 2),
        [tiles(piece, chans, F32)] + [tiles(piece, chans, BF16)] * (size - 1),
        [keep_two, got_two, keep_one, got_one],
        scalars=[digit],
        name="join",
    )
    got = [swap_to(s, stride, size, i + 1, devices) for i, s in enumerate(sends)]
    order = [conv_out([kept])]
    block_out = order[0]
    d_edges = None
    for (stride, size), digit in zip(stages[1:], digits[1:]):
        piece = kept.shape[0] // size
        carried = [] if d_edges else [grad_pre[:1], grad_pre[planes - 1 :]]
        outs = call(
            functools.partial(scatter_kernel, size, len(got), len(carried)),
            [tiles(piece, chans, F32)] + [tiles(piece, chans, BF16)] * (size - 1) + [plane] * len(carried),
            [kept, *got, *carried],
            scalars=[digit],
            order=order,
            name="scatter",
        )
        kept, sends = outs[0], outs[1:size]
        got = [swap_to(s, stride, size, i + 1, devices) for i, s in enumerate(sends)]
        if carried:
            d_edges = from_sides(*outs[size:])
        order = []
    (mine,) = call(
        functools.partial(scatter_kernel, 1, len(got), 0),
        [tiles(kept.shape[0], chans, BF16)],
        [kept, *got],
        scalars=[digits[0]],
        name="sum",
    )
    input_grad = conv_in([mine], *d_edges)
    order = [input_grad]
    for (stride, size), digit in list(zip(stages, digits))[:0:-1]:
        pieces = [mine] + [swap_to(mine, stride, size, o, devices) for o in range(1, size)]
        (mine,) = call(
            functools.partial(gather_kernel, size),
            [tiles(size * mine.shape[0], chans, BF16)],
            pieces,
            scalars=[digit],
            order=order,
            name="gather",
        )
        order = []
    (stride, size), digit = stages[0], digits[0]
    pieces = [mine] + [swap_to(mine, stride, size, o, devices) for o in range(1, size)]
    others = [swap_to(p, space, 2, 1, devices) for p in pieces]
    factor = 1.0 / math.sqrt(devices * planes * rows)
    grad_one, grad_two = call(
        functools.partial(finish_kernel, size, half // size, factor),
        [tiles(2 * half, chans, F32)] * 2,
        pieces + others,
        scalars=[core, digit],
        name="finish",
    )[::-1]
    shape = filter_one.shape
    return (
        block_out.reshape(volume.shape),
        input_grad.reshape(volume.shape),
        grad_one.reshape(shape),
        grad_two.reshape(shape),
    )


def solution(mesh):
    cells, whole = P("dp", "space", None, None, None), P()
    return jax.shard_map(
        local,
        mesh=mesh,
        in_specs=(cells, whole, whole, cells),
        out_specs=(cells, cells, whole, whole),
        check_vma=False,
    )
```

```python
import functools
import math

import jax
import jax.numpy as jnp
from jax import lax
from jax.experimental import pallas as pl
from jax.experimental.pallas import tpu as pltpu
from jax.sharding import PartitionSpec as P

AXES = ("dp", "space")
LIMIT = 20 * 2**20
VMEM = pl.BlockSpec(memory_space=pltpu.VMEM)
ANY = pl.BlockSpec(memory_space=pl.ANY)
BF16, F32 = jnp.bfloat16, jnp.float32


def divisor(n, most):
    return max(d for d in range(1, most + 1) if n % d == 0)


def factors(n):
    out = []
    while n > 1:
        f = 4 if n % 4 == 0 else 2
        out.append(f)
        n //= f
    return out


def swap_to(value, stride, size, offset, devices):
    def partner(rank):
        digit = (rank // stride) % size
        return rank + ((digit ^ offset) - digit) * stride

    return lax.ppermute(value, AXES, [(rank, partner(rank)) for rank in range(devices)])


def call(kernel, outs, args, scalars=(), order=(), scratch=(), flops=0, name=None):
    size = sum(a.size * a.dtype.itemsize for a in args) + sum(o.size * o.dtype.itemsize for o in outs)
    used = len(args)

    def body(*refs):
        rank = lax.axis_index("dp") * lax.axis_size("space") + lax.axis_index("space")
        kernel(*[[scalar(rank)] for scalar in scalars], *refs[:used], *refs[used + len(order) :])

    return pl.pallas_call(
        body,
        out_shape=list(outs),
        in_specs=[VMEM] * len(args) + [ANY] * len(order),
        out_specs=[VMEM] * len(outs),
        scratch_shapes=list(scratch),
        cost_estimate=pl.CostEstimate(flops=flops, bytes_accessed=size, transcendentals=0),
        compiler_params=pltpu.CompilerParams(vmem_limit_bytes=LIMIT),
        name=name,
    )(*args, *order)


def blocks(count, most, body):
    step = divisor(count, most)

    def one(i, carry):
        body(pl.multiple_of(i * step, step), step)
        return carry

    lax.fori_loop(0, count // step, one, 0)


def copy(source, target):
    target[...] = source[...]


def tiles(count, chans, dtype):
    return jax.ShapeDtypeStruct((count, 8, chans), dtype)


def join_kernel(size, pairs, digit_ref, *refs):
    given, rest = refs[: 2 * pairs], refs[2 * pairs :]
    part = given[0].shape[0] // size
    digit = digit_ref[0]
    for offset in range(size):
        target = rest[offset]
        for pair in range(pairs):
            kept, got = given[2 * pair], given[2 * pair + 1]

            def move(at, step, kept=kept, got=got, target=target, pair=pair, offset=offset):
                here = pl.ds((digit ^ offset) * part + at, step)
                value = kept[here] + got[here].astype(F32)
                target[pl.ds(pair * part + at, step)] = value.astype(target.dtype)

            blocks(part, 32, move)
        spare = target.shape[0] - pairs * part
        if spare:
            target[pl.ds(pairs * part, spare)] = jnp.zeros((spare,) + target.shape[1:], target.dtype)


def scatter_kernel(size, arrived, carried, digit_ref, *refs):
    kept, got = refs[0], refs[1 : 1 + arrived]
    moved = refs[1 + arrived : 1 + arrived + carried]
    outs = refs[1 + arrived + carried :]
    for source, target in zip(moved, outs[size:]):
        copy(source, target)
    digit = digit_ref[0]
    piece = outs[0].shape[0]
    for offset in range(size):
        base = (digit ^ offset) * piece if size > 1 else 0

        def move(at, step, base=base, target=outs[offset]):
            value = kept[pl.ds(base + at, step)]
            for other in got:
                value = value + other[pl.ds(base + at, step)].astype(F32)
            target[pl.ds(at, step)] = value.astype(target.dtype)

        blocks(piece, 32, move)


def gather_kernel(size, digit_ref, *refs):
    out = refs[size]
    digit = digit_ref[0]
    piece = refs[0].shape[0]
    for offset in range(size):
        base = (digit ^ offset) * piece

        def move(at, step, base=base, source=refs[offset]):
            out[pl.ds(base + at, step)] = source[pl.ds(at, step)]

        blocks(piece, 32, move)


def finish_kernel(size, part, factor, core_ref, digit_ref, *refs):
    outs = refs[2 * size :]
    half = size * part
    for side in range(2):
        core = core_ref[0] ^ side
        for offset in range(size):
            source = refs[side * size + offset]
            for i, out in enumerate(outs):

                def move(at, step, source=source, out=out, core=core, offset=offset, i=i):
                    to = core * half + (digit_ref[0] ^ offset) * part + at
                    out[pl.ds(to, step)] = source[pl.ds(i * part + at, step)].astype(F32) * factor

                blocks(part, 32, move)


def turn_kernel(one_ref, two_ref, one_out, two_out):
    for source, target in ((one_ref, one_out), (two_ref, two_out)):
        chans = source.shape[1]
        taps = source.shape[0] // chans

        def turn(tap, carry, source=source, target=target, taps=taps, chans=chans):
            block = source[pl.ds(pl.multiple_of((taps - 1 - tap) * chans, chans), chans), :]
            to = pl.ds(pl.multiple_of(tap * chans, chans), chans)
            target[to, :] = jnp.transpose(block.astype(F32)).astype(BF16)
            return carry

        lax.fori_loop(0, taps, turn, 0, unroll=3)


def spread(source, plane, wide, slot, side):
    chans = source.shape[-1]
    step = 8 * side
    edge = jnp.zeros((side, 3 * chans), BF16)
    wide[slot, pl.ds(0, side), :] = edge
    wide[slot, pl.ds(side + source.shape[1], side), :] = edge
    column = lax.broadcasted_iota(jnp.int32, (step, chans), 0) % side

    def some(i, carry):
        at = pl.multiple_of(i * step, step)
        value = source[plane, pl.ds(at, step), :]
        full = value.astype(F32)
        left = jnp.where(column == 0, 0.0, pltpu.roll(full, 1, 0))
        right = jnp.where(column == side - 1, 0.0, pltpu.roll(full, step - 1, 0))
        to = pl.ds(pl.multiple_of(at + side, side), step)
        wide[slot, to, pl.ds(0, chans)] = left.astype(BF16)
        wide[slot, to, pl.ds(chans, chans)] = value
        wide[slot, to, pl.ds(2 * chans, chans)] = right.astype(BF16)
        return carry

    lax.fori_loop(0, source.shape[1] // step, some, 0)


def spread_all(odd, own, near, far, wide, side):
    planes = own.shape[0]
    for plane in range(planes):
        spread(own, plane, wide, plane + 1, side)
    spread(near, 0, wide, (planes + 1) * (1 - odd), side)
    spread(far, 0, wide, (planes + 1) * odd, side)


def conv(wide, weights, side, finish):
    slots, rows = wide.shape[0], wide.shape[1] - 2 * side
    planes, chans = slots - 2, weights.shape[1]
    depth = 9 * chans
    step = STEP * side
    empty = jnp.zeros((depth, chans), BF16)

    def some(i, carry):
        at = pl.multiple_of(i * step, step)
        left = jnp.concatenate(
            [
                wide[slot, pl.ds(pl.multiple_of(at + dy * side, side), step), :]
                for slot in range(slots)
                for dy in range(3)
            ],
            axis=-1,
        )
        right = jnp.concatenate(
            [
                jnp.concatenate(
                    [
                        weights[pl.ds((slot - out) * depth, depth), :] if 0 <= slot - out <= 2 else empty
                        for out in range(planes)
                    ],
                    axis=-1,
                )
                for slot in range(slots)
            ],
            axis=0,
        )
        sums = jnp.dot(left, right, preferred_element_type=F32)
        for plane in range(planes):
            finish(plane, pl.ds(at, step), sums[:, plane * chans : (plane + 1) * chans])
        return carry

    lax.fori_loop(0, rows // step, some, 0)


def silu_kernel(side, odd_ref, own, near, far, weights, wide, act, to_near, to_far, slope):
    odd = odd_ref[0]
    spread_all(odd, own, near, far, wide, side)

    def finish(plane, at, pre):
        sigma = 1.0 / (1.0 + jnp.exp(-pre))
        value = (pre * sigma).astype(BF16)
        act[plane, at, :] = value
        slope[plane, at, :] = sigma * (1.0 + pre * (1.0 - sigma))

    conv(wide, weights, side, finish)
    ends(odd, act, to_near, to_far)


def slope_kernel(side, odd_ref, own, near, far, weights, slope, wide, grad):
    spread_all(odd_ref[0], own, near, far, wide, side)

    def finish(plane, at, part):
        grad[plane, at, :] = (part * slope[plane, at, :]).astype(BF16)

    conv(wide, weights, side, finish)


def add_kernel(side, odd_ref, own, near, far, weights, base, out, wide):
    spread_all(odd_ref[0], own, near, far, wide, side)

    def finish(plane, at, part):
        out[plane, at, :] = (base[plane, at, :].astype(F32) + part).astype(BF16)

    conv(wide, weights, side, finish)


def outer_kernel(turned, core_ref, odd_ref, own, wide, keep, send, *rest):
    planes, rows, chans = own.shape
    side = (wide.shape[1] - rows) // 2
    flat, sums, full = rest[-3:]
    if len(rest) > 3:
        ends(odd_ref[0], own, *rest[:2])
    for plane in range(planes):
        for i in range(rows // 256):
            value = own[plane, pl.ds(i * 256, 256), :].astype(F32)
            flat[pl.ds(plane * chans, chans), pl.ds(i * 256, 256)] = jnp.transpose(value).astype(BF16)
    for slot in range(planes + 2):
        begin, end = max(0, slot - 2), min(planes, slot + 1)
        right = jnp.concatenate([wide[slot, pl.ds(dy * side, rows), :] for dy in range(3)], axis=-1)
        left = flat[pl.ds(begin * chans, (end - begin) * chans), :]
        product = jnp.dot(left, right, preferred_element_type=F32)
        for plane in range(begin, end):
            part = product[(plane - begin) * chans : (plane - begin + 1) * chans]
            sums[slot - plane] = part if plane == 0 else sums[slot - plane] + part
    deep = chans // 8
    for kz in range(3):
        for tap in range(9):
            part = sums[kz, :, pl.ds(tap * chans, chans)]
            index = kz * 9 + tap if turned else 26 - kz * 9 - tap
            part = jnp.transpose(part) if turned else part
            full[pl.ds(index * deep, deep)] = part.reshape(deep, 8, chans)
    half = keep.shape[0]
    for target, core in ((keep, core_ref[0]), (send, 1 - core_ref[0])):

        def move(at, step, target=target, core=core):
            target[pl.ds(at, step)] = full[pl.ds(core * half + at, step)].astype(target.dtype)

        blocks(half, 32, move)


def ends(odd, cells, to_near, to_far):
    last = cells.shape[0] - 1
    to_near[0] = cells[last * (1 - odd)]
    to_far[0] = cells[last * odd]


def edge_kernel(odd_ref, cells, to_near, to_far):
    ends(odd_ref[0], cells, to_near, to_far)


class Places:
    def __init__(self, dp, space):
        self.dp, self.space = dp, space
        self.even = dp % 2 == 0 and space % 2 == 0

    def other(self, rank):
        sample, slab = rank // self.space, rank % self.space
        if not self.even:
            return rank
        low, bit = sample % 2, slab % 2
        return (sample - low + bit) * self.space + slab - bit + low

    def move(self, value):
        pairs = [(rank, self.other(rank)) for rank in range(self.dp * self.space)]
        return lax.ppermute(value, AXES, pairs)

    def shift(self, value, links):
        pairs = [
            (self.other(sample * self.space + a), self.other(sample * self.space + b))
            for sample in range(self.dp)
            for i, j in links
            for a, b in ((i, j), (j, i))
        ]
        return lax.ppermute(value, AXES, pairs)

    def sides(self, to_near, to_far):
        near = self.shift(to_near, [(i, i + 1) for i in range(0, self.space - 1, 2)])
        far = self.shift(to_far, [(i, i + 1) for i in range(1, self.space - 1, 2)])
        return near, far


STEP = 32


def local(volume, filter_one, filter_two, cotangent):
    _, planes, side, _, chans = volume.shape
    rows = side * side
    dp, space = lax.axis_size("dp"), lax.axis_size("space")
    devices = dp * space

    def digit_of(stride, size):
        return lambda rank: (rank // stride) % size

    core = digit_of(space, 2)
    places = Places(dp, space)
    odd = core if places.even else digit_of(1, 2)
    w_one = filter_one.reshape(-1, chans)
    w_two = filter_two.reshape(-1, chans)
    slab = jax.ShapeDtypeStruct((planes, rows, chans), BF16)
    plane = jax.ShapeDtypeStruct((1, rows, chans), BF16)
    wide = jax.ShapeDtypeStruct((planes + 2, rows + 2 * side, 3 * chans), BF16)
    flops = 2 * planes * rows * 27 * chans * chans
    half = 27 * chans // 16

    stages, stride = [], 1
    for size in factors(space):
        stages.append((stride, size))
        stride *= size
    stride = 2 * space
    for size in factors(dp // 2):
        stages.append((stride, size))
        stride *= size
    digits = [digit_of(stride, size) for stride, size in stages]

    field = places.move(volume.reshape(planes, rows, chans))
    grad_out = places.move(cotangent.reshape(planes, rows, chans))
    back_one, back_two = call(
        turn_kernel, [jax.ShapeDtypeStruct(w_one.shape, BF16)] * 2, [w_one, w_two], name="turn"
    )
    near_x, far_x = places.sides(*call(edge_kernel, [plane] * 2, [field], [odd], [back_two], name="edges_x"))
    near_g, far_g = places.sides(*call(edge_kernel, [plane] * 2, [grad_out], [odd], name="edges_g"))
    wide_x, act, *a_ends, slope = call(
        functools.partial(silu_kernel, side),
        [wide, slab, plane, plane, jax.ShapeDtypeStruct(slab.shape, F32)],
        [field, near_x, far_x, w_one],
        [odd],
        flops=flops,
        name="conv_pre",
    )
    near_a, far_a = places.sides(*a_ends)
    wide_g, grad_pre = call(
        functools.partial(slope_kernel, side),
        [wide, slab],
        [grad_out, near_g, far_g, back_two, slope],
        [odd],
        flops=flops,
        name="conv_act_grad",
    )

    def outer(turned, own, spread_out, order, name):
        return call(
            functools.partial(outer_kernel, turned),
            [tiles(half, chans, F32)] * 2 + [plane] * (2 if turned else 0),
            [own, spread_out],
            scalars=[core, odd],
            order=order,
            scratch=[
                pltpu.VMEM((planes * chans, rows), BF16),
                pltpu.VMEM((3, chans, 9 * chans), F32),
                pltpu.VMEM((2 * half, 8, chans), F32),
            ],
            flops=flops,
            name=name,
        )

    keep_two, send_two = outer(False, act, wide_g, [near_a, far_a], "outer_two")
    got_two = swap_to(send_two, space, 2, 1, devices)
    keep_one, send_one, *d_ends = outer(True, grad_pre, wide_x, [send_two], "outer_one")
    got_one = swap_to(send_one, space, 2, 1, devices)
    near_d, far_d = places.sides(*d_ends)

    def conv_out(order):
        return call(
            functools.partial(add_kernel, side),
            [slab],
            [act, near_a, far_a, w_two, field],
            [odd],
            order=order,
            scratch=[pltpu.VMEM(wide.shape, BF16)],
            flops=flops,
            name="conv_out",
        )[0]

    def conv_in(order):
        return call(
            functools.partial(add_kernel, side),
            [slab],
            [grad_pre, near_d, far_d, back_one, grad_out],
            [odd],
            order=order,
            scratch=[pltpu.VMEM(wide.shape, BF16)],
            flops=flops,
            name="conv_in",
        )[0]

    (stride, size), digit = stages[0], digits[0]
    rest = devices // 2 // size
    piece = -(-2 * half // size // rest) * rest
    kept, *sends = call(
        functools.partial(join_kernel, size, 2),
        [tiles(piece, chans, F32)] + [tiles(piece, chans, BF16)] * (size - 1),
        [keep_two, got_two, keep_one, got_one],
        scalars=[digit],
        name="join",
    )
    got = [swap_to(s, stride, size, i + 1, devices) for i, s in enumerate(sends)]
    moved = [conv_out([kept])]
    for (stride, size), digit in zip(stages[1:], digits[1:]):
        piece = kept.shape[0] // size
        outs = call(
            functools.partial(scatter_kernel, size, len(got), len(moved)),
            [tiles(piece, chans, F32)] + [tiles(piece, chans, BF16)] * (size - 1) + [slab] * len(moved),
            [kept, *got, *moved],
            scalars=[digit],
            name="scatter",
        )
        kept, sends = outs[0], outs[1:size]
        got = [swap_to(s, stride, size, i + 1, devices) for i, s in enumerate(sends)]
        if moved:
            block_out = places.move(outs[size])
            moved = []
    input_grad = conv_in([kept])
    (mine,) = call(
        functools.partial(scatter_kernel, 1, len(got), 0),
        [tiles(kept.shape[0], chans, BF16)],
        [kept, *got],
        scalars=[digits[0]],
        order=[input_grad],
        name="sum",
    )
    input_grad = places.move(input_grad)
    order = []
    for (stride, size), digit in list(zip(stages, digits))[:0:-1]:
        pieces = [mine] + [swap_to(mine, stride, size, o, devices) for o in range(1, size)]
        (mine,) = call(
            functools.partial(gather_kernel, size),
            [tiles(size * mine.shape[0], chans, BF16)],
            pieces,
            scalars=[digit],
            order=order,
            name="gather",
        )
        order = []
    (stride, size), digit = stages[0], digits[0]
    pieces = [mine] + [swap_to(mine, stride, size, o, devices) for o in range(1, size)]
    others = [swap_to(p, space, 2, 1, devices) for p in pieces]
    factor = 1.0 / math.sqrt(devices * planes * rows)
    grad_one, grad_two = call(
        functools.partial(finish_kernel, size, half // size, factor),
        [tiles(2 * half, chans, F32)] * 2,
        pieces + others,
        scalars=[core, digit],
        name="finish",
    )[::-1]
    shape = filter_one.shape
    return (
        block_out.reshape(volume.shape),
        input_grad.reshape(volume.shape),
        grad_one.reshape(shape),
        grad_two.reshape(shape),
    )


def solution(mesh):
    cells, whole = P("dp", "space", None, None, None), P()
    return jax.shard_map(
        local,
        mesh=mesh,
        in_specs=(cells, whole, whole, cells),
        out_specs=(cells, cells, whole, whole),
        check_vma=False,
    )
```
